512 devices in a mesh: section: 32 (over y_hi, z), dp: 16 (over x, y_lo, core).
Axes of the slice: x: 4, y: 8 (y_hi: 4, y_lo: 2; y = y_hi * 2 + y_lo), z: 8, core: 2. Of those that a mesh axis runs over, the one named last changes fastest.
Arguments:
- checkpoints: bfloat16 [32, 3, 64, 1024], P('section', None, None, 'dp'), may hold values from -6 to 6
- gain: float32 [32, 1024], P('section'), may hold values from 0.25 to 1.75
- w_in: bfloat16 [32, 1024, 8192], P('section', None, 'dp'), may hold values from -0.09375 to 0.09375
- w_out: bfloat16 [32, 8192, 1024], P('section', 'dp'), may hold values from -0.0625 to 0.0625
- cotangent: bfloat16 [3, 64, 4096], P(None, None, 'dp'), may hold values from -6 to 6
Outputs:
- grad_in: bfloat16 [32, 1024, 8192], P('section', None, 'dp')
- grad_out: bfloat16 [32, 8192, 1024], P('section', 'dp')
- grad_gain: float32 [32, 1024], P('section', 'dp')
- section_grads: bfloat16 [32, 3, 64, 1024], P('section', None, None, 'dp')
The draws below stay inside these ranges and needn't reach their ends.
All inputs are finite; a program needn't handle non-finite values.
Results may differ from the reference program's by a relative error of at most 0.04.
Values may be sent and summed in bfloat16 or wider, within the bound.
A program may use at most 64 MiB of HBM per device.

```python
import jax
import jax.numpy as jnp
from jax import lax

D = 4096
FF = 8192
TOK = 64
MICRO = 3
QD = 1024
LAYERS = 8
N_SECTION = 32
N_DP = 16


def steps_of(own_key, extent, cuts, smallest, top_value):
    level, own = 1.0, jax.random.fold_in(own_key, 6)
    for axis_at, shards_of in cuts:
        heights = jnp.exp(jax.random.uniform(jax.random.fold_in(own, axis_at), (shards_of,), jnp.float32, smallest / len(cuts), top_value / len(cuts)))
        level = level * jnp.repeat(heights, extent[axis_at] // shards_of).reshape([-1 if axis == axis_at else 1 for axis in range(len(extent))])
    return level


def centred(stream_key, shape, deviation, most, split=(), kind=jnp.bfloat16):
    drawn = jax.random.normal(stream_key, shape, jnp.float32) * deviation
    if len(split) > 0:
        drawn = steps_of(stream_key, shape, split, -0.22, 0.18) * drawn
    return jnp.clip(drawn, min=-most, max=most).astype(kind)


def setup_inputs(seed: int = 0) -> dict:
    seeds = jax.random.split(jax.random.key(seed), 6)
    checkpoints = centred(seeds[0], (N_SECTION, MICRO, TOK, QD), 1.0, 6.0, ((0, 32), (3, 16)))
    gain = jnp.clip(1.0 + 0.15 * jax.random.normal(seeds[1], (N_SECTION, QD), jnp.float32), 0.25, 1.75)
    w_in = centred(seeds[2], (N_SECTION, QD, FF), D ** -0.5, 0.09375, ((0, 32), (2, 16)))
    w_out = centred(seeds[3], (N_SECTION, FF, QD), FF ** -0.5, 0.0625, ((0, 32), (1, 16)))
    cotangent = centred(seeds[4], (MICRO, TOK, D), 1.0, 6.0, ((2, 16),))
    return dict(checkpoints=checkpoints, gain=gain, w_in=w_in, w_out=w_out, cotangent=cotangent)


def gelu_tanh(value):
    return jax.nn.gelu(value, approximate=True)

def layer_back(x_saved, gain_row, weight_in, weight_out, grad_b):
    x_full = x_saved.astype(jnp.float32)
    scale = lax.rsqrt(lax.optimization_barrier(jnp.mean(x_full * x_full, axis=-1, keepdims=True)) + 1e-06)
    normed = x_full * scale
    scaled = (normed * gain_row).astype(jnp.bfloat16)
    act = jnp.dot(scaled, weight_in, preferred_element_type=jnp.float32)
    hidden, pull = jax.vjp(gelu_tanh, act)
    hidden_b = hidden.astype(jnp.bfloat16)
    dhid = jnp.dot(grad_b, weight_out.T, preferred_element_type=jnp.float32)
    dact = pull(dhid)[0].astype(jnp.bfloat16)
    gout = jnp.dot(hidden_b.T, grad_b, preferred_element_type=jnp.float32)
    gin = jnp.dot(scaled.T, dact, preferred_element_type=jnp.float32)
    share = FF // N_DP
    pieces = jnp.einsum('tnf,enf->nte', dact.astype(jnp.float32).reshape(TOK, N_DP, share), weight_in.astype(jnp.float32).reshape(D, N_DP, share))
    rounded = lax.optimization_barrier(pieces.astype(jnp.bfloat16))
    dnorm_in = lax.optimization_barrier(jnp.sum(rounded.astype(jnp.float32), axis=0))
    dnorm = dnorm_in * gain_row
    inner = lax.optimization_barrier(jnp.mean(dnorm * normed, axis=-1, keepdims=True))
    grad_x = (grad_b.astype(jnp.float32) + scale * (dnorm - normed * inner)).astype(jnp.bfloat16)
    dgain = lax.optimization_barrier(jnp.sum(dnorm_in * normed, axis=0))
    return (grad_x, gin, gout, dgain)

def reference(checkpoints, gain, w_in, w_out, cotangent):
    saved_all = checkpoints.reshape(LAYERS, 4, MICRO, TOK, QD).transpose(0, 2, 3, 1, 4).reshape(LAYERS, MICRO, TOK, D)
    gain_all = gain.reshape(LAYERS, D)
    win_all = w_in.reshape(LAYERS, D, FF)
    wout_all = w_out.reshape(LAYERS, 4, FF, QD).transpose(0, 2, 1, 3).reshape(LAYERS, FF, D)

    def one_section(grads, items):
        saved, gain_row, weight_in, weight_out = items

        def one_micro(pair):
            return layer_back(pair[0], gain_row, weight_in, weight_out, pair[1])
        grad_x, gin, gout, dgain = lax.map(one_micro, (saved, grads))
        result = (grad_x, lax.optimization_barrier(jnp.sum(gin, axis=0)).astype(jnp.bfloat16), lax.optimization_barrier(jnp.sum(gout, axis=0)).astype(jnp.bfloat16), lax.optimization_barrier(jnp.sum(dgain, axis=0)))
        return (grad_x, result)
    items = (saved_all[::-1], gain_all[::-1], win_all[::-1], wout_all[::-1])
    final, stacked = lax.scan(one_section, cotangent, items)
    grad_x, gin, gout, dgain = stacked
    gin = gin[::-1].reshape(N_SECTION, QD, FF)
    gout = gout[::-1].reshape(LAYERS, FF, 4, QD).transpose(0, 2, 1, 3).reshape(N_SECTION, FF, QD)
    dgain = dgain[::-1].reshape(N_SECTION, QD)
    grad_x = grad_x[::-1].reshape(LAYERS, MICRO, TOK, 4, QD).transpose(0, 3, 1, 2, 4).reshape(N_SECTION, MICRO, TOK, QD)
    return (gin, gout, dgain, grad_x)
```

```python
import functools

import jax
import jax.numpy as jnp
from jax import lax
from jax.experimental import pallas as pl
from jax.experimental.pallas import tpu as pltpu
from jax.sharding import PartitionSpec as P

MESH = pl.DeviceIdType.MESH
F32 = jnp.float32
BF16 = jnp.bfloat16
K0 = 0.7978845608028654
K1 = 0.044715


def dot_nn(a, b):
    return lax.dot_general(a, b, (((1,), (0,)), ((), ())), preferred_element_type=F32)


def dot_nt(a, b):
    return lax.dot_general(a, b, (((1,), (1,)), ((), ())), preferred_element_type=F32)


def dot_tn(a, b):
    return lax.dot_general(a, b, (((0,), (0,)), ((), ())), preferred_element_type=F32)


def chain(
    sizes,
    x_ref, cot_ref, gain_ref, win_ref, wout_ref,
    gin_ref, gout_ref, gg_ref, dxo_ref,
    xsib, xs, xg, dy, shin, rs, qs, dxs, dxsib,
    a1s, a1r, a2s, a2r, apart, sqs, act, slope, hid, dact, ub, rb,
    d1s, d1r, d2s, d2r, dpart, ggacc, ggr,
    sem1, semw,
):
    waves, rows, width, quarter, hidden, sections, peers = sizes
    half = rows // 2
    s = lax.axis_index("section")
    d = lax.axis_index("dp")
    layer, j = s // 4, s % 4
    top = sections // 4 - 1
    g, c = d // 2, d % 2
    sib = d + 1 - 2 * c
    near = s + 1 - 2 * (s % 2)
    far = s + 2 - 4 * ((s // 2) % 2)
    below = (s + sections - 4) % sections
    above = (s + 4) % sections

    def at(section, dp):
        return {"section": section, "dp": dp}

    def remote(src, dst, send, recv, section, dp):
        return pltpu.make_async_remote_copy(
            src_ref=src, dst_ref=dst, send_sem=send, recv_sem=recv,
            device_id=at(section, dp), device_id_type=MESH,
        )

    def take(ref, sem):
        pltpu.make_async_copy(ref, ref, sem).wait()

    barrier = pltpu.get_barrier_semaphore()
    for k in range(1, peers):
        pl.semaphore_signal(barrier, inc=1, device_id=at(s, (d + k) % peers), device_id_type=MESH)
    for other in (near, far, below, above):
        pl.semaphore_signal(barrier, inc=1, device_id=at(other, d), device_id_type=MESH)
    pl.semaphore_wait(barrier, peers + 3)

    SX, RX, SC, SP, RP, SG, RG = range(7)
    (S_XG, R_XG, S_A1, R_A1, S_A2, R_A2, S_SH, R_SH, S_DY, R_DY,
     S_D1, R_D1, S_D2, R_D2, S_RS, R_RS) = range(16)

    own_rows = pl.ds(pl.multiple_of(c * half, half), half)
    own_cols = pl.ds(pl.multiple_of(g * 128, 128), 128)

    pair = remote(x_ref, xsib, sem1.at[SX], sem1.at[RX], s, sib)
    pair.start()

    per = width // quarter
    q = d % per
    holds_cot = (layer == top) & (d // per == j)

    def cot_copies(w, start):
        for b in range(2):
            for hf in range(2):
                owner = q * 4 + b * 2 + hf
                src = cot_ref.at[w, pl.ds(hf * half, half), pl.ds(b * 128, 128)]
                dst = shin.at[w]

                @pl.when(owner == d)
                def _():
                    copy = pltpu.make_async_copy(src, dst, semw.at[R_SH, w])
                    if start:
                        copy.start()

                @pl.when(owner != d)
                def _():
                    copy = remote(src, dst, sem1.at[SC], semw.at[R_SH, w], s, owner)
                    if start:
                        copy.start()
                    else:
                        copy.wait_send()

    @pl.when(holds_cot)
    def _():
        for w in range(waves):
            cot_copies(w, True)

    pair.wait_recv()

    def to_everyone(src, buf, send, recv, w):
        dst = buf.at[w, own_rows, own_cols]
        for k in range(1, peers):
            remote(src, dst, semw.at[send, w], semw.at[recv, w], s, (d + k) % peers).start()
        pltpu.make_async_copy(src, dst, semw.at[recv, w]).start()

    def sent_to_everyone(send, w):
        take(rs.at[w, pl.ds(1, peers - 1)], semw.at[send, w])

    @pl.loop(0, waves)
    def _(w):
        xs[w] = x_ref[w] + xsib[w]
        to_everyone(xs.at[w, own_rows], xg, S_XG, R_XG, w)

    gain = gain_ref[...]

    @pl.loop(0, waves)
    def _(w):
        take(xg.at[w], semw.at[R_XG, w])
        xf = xg[w].astype(F32)
        sq = jnp.sum(xf * xf, axis=-1, keepdims=True)
        sq = jnp.broadcast_to(sq, (rows, 128))
        part = dot_nn((xf * gain).astype(BF16), win_ref[...])
        apart[w] = part
        sqs[w] = sq
        a1s[w, :, :hidden] = part.astype(BF16)
        a1s[w, :, hidden:] = sq.astype(BF16)
        remote(a1s.at[w], a1r.at[w], semw.at[S_A1, w], semw.at[R_A1, w], near, d).start()

    @pl.loop(0, waves)
    def _(w):
        take(a1r.at[w], semw.at[R_A1, w])
        part = apart[w] + a1r[w, :, :hidden].astype(F32)
        sq = sqs[w] + a1r[w, :, hidden:].astype(F32)
        apart[w] = part
        sqs[w] = sq
        a2s[w, :, :hidden] = part.astype(BF16)
        a2s[w, :, hidden:] = sq.astype(BF16)
        remote(a2s.at[w], a2r.at[w], semw.at[S_A2, w], semw.at[R_A2, w], far, d).start()

    @pl.loop(0, waves)
    def _(w):
        take(a2r.at[w], semw.at[R_A2, w])
        part = apart[w] + a2r[w, :, :hidden].astype(F32)
        sq = sqs[w] + a2r[w, :, hidden:].astype(F32)
        r = lax.rsqrt(sq / width + 1e-06)
        rb[w] = r
        r1 = r[:, :1]
        a = part * r1
        t = jnp.tanh(K0 * (a + K1 * a * a * a))
        act[w] = a
        hid[w] = (0.5 * a * (1.0 + t)).astype(BF16)
        slope[w] = 0.5 * (1.0 + t) + 0.5 * a * (1.0 - t * t) * (K0 * (1.0 + 3.0 * K1 * a * a))
        ub[w] = (xg[w].astype(F32) * r1 * gain).astype(BF16)

    ggacc[...] = jnp.zeros_like(ggacc)

    @pl.loop(0, waves)
    def _(w):
        take(shin.at[w], semw.at[R_SH, w])
        to_everyone(shin.at[w], dy, S_DY, R_DY, w)

    @pl.loop(0, waves)
    def _(w):
        take(dy.at[w], semw.at[R_DY, w])
        part = dot_nt(dy[w], wout_ref[...])
        dpart[w] = part
        d1s[w] = part.astype(BF16)
        remote(d1s.at[w], d1r.at[w], semw.at[S_D1, w], semw.at[R_D1, w], near, d).start()

    @pl.loop(0, waves)
    def _(w):
        take(d1r.at[w], semw.at[R_D1, w])
        part = dpart[w] + d1r[w].astype(F32)
        dpart[w] = part
        d2s[w] = part.astype(BF16)
        remote(d2s.at[w], d2r.at[w], semw.at[S_D2, w], semw.at[R_D2, w], far, d).start()

    @pl.loop(0, waves)
    def _(w):
        take(d2r.at[w], semw.at[R_D2, w])
        dh = dpart[w] + d2r[w].astype(F32)
        da = (slope[w] * dh).astype(BF16)
        dact[w] = da
        r1 = rb[w, :, :1]
        mean = jnp.sum(da.astype(F32) * act[w], axis=-1, keepdims=True) / width
        p = dot_nt(da, win_ref[...])
        xf = xg[w].astype(F32)
        n = xf * r1
        ggacc[...] += jnp.broadcast_to(jnp.sum(p * n, axis=0, keepdims=True), ggacc.shape)
        qs[w] = ((p * gain - n * mean) * r1).astype(BF16)
        for k in range(1, peers):
            e = (d + k) % peers
            src = qs.at[w, pl.ds(pl.multiple_of(e % 2 * half, half), half),
                        pl.ds(pl.multiple_of(e // 2 * 128, 128), 128)]
            remote(src, rs.at[w, k], semw.at[S_RS, w], semw.at[R_RS, w], s, e).start()
        pltpu.make_async_copy(qs.at[w, own_rows, own_cols], rs.at[w, 0], semw.at[R_RS, w]).start()

    @pl.loop(0, waves)
    def _(w):
        take(rs.at[w], semw.at[R_RS, w])
        total = dy[w, own_rows, own_cols].astype(F32)
        for k in range(peers):
            total = total + rs[w, k].astype(F32)
        dxs[w] = total.astype(BF16)

        @pl.when(layer > 0)
        def _():
            remote(dxs.at[w], shin.at[w], semw.at[S_SH, w], semw.at[R_SH, w], below, d).start()

    share = remote(dxs, dxsib, sem1.at[SP], sem1.at[RP], s, sib)
    share.start()
    for k in range(1, peers):
        e = (d + k) % peers
        src = ggacc.at[:, pl.ds(pl.multiple_of(e // 2 * 128, 128), 128)]
        remote(src, ggr.at[k], sem1.at[SG], sem1.at[RG], s, e).start()
    pltpu.make_async_copy(ggacc.at[:, own_cols], ggr.at[0], sem1.at[RG]).start()

    tokens = waves * rows
    gout_ref[...] = dot_tn(hid[...].reshape(tokens, hidden), dy[...].reshape(tokens, quarter)).astype(BF16)
    gin_ref[...] = dot_tn(ub[...].reshape(tokens, quarter), dact[...].reshape(tokens, hidden)).astype(BF16)

    take(ggr, sem1.at[RG])
    gg = ggr[0]
    for k in range(1, peers):
        gg = gg + ggr[k]
    gg_ref[...] = gg
    share.wait_recv()
    other_rows = pl.ds(pl.multiple_of((1 - c) * half, half), half)
    for w in range(waves):
        dxo_ref[w, own_rows, :] = dxs[w]
        dxo_ref[w, other_rows, :] = dxsib[w]

    pair.wait_send()
    share.wait_send()
    take(ggr.at[pl.ds(1, peers - 1)], sem1.at[SG])

    @pl.when(holds_cot)
    def _():
        for w in range(waves):
            cot_copies(w, False)

    @pl.loop(0, waves)
    def _(w):
        sent_to_everyone(S_XG, w)
        sent_to_everyone(S_DY, w)
        sent_to_everyone(S_RS, w)
        take(a1s.at[w], semw.at[S_A1, w])
        take(a2s.at[w], semw.at[S_A2, w])
        take(d1s.at[w], semw.at[S_D1, w])
        take(d2s.at[w], semw.at[S_D2, w])

        @pl.when(layer > 0)
        def _():
            take(dxs.at[w], semw.at[S_SH, w])


def shards(checkpoints, gain, w_in, w_out, cotangent):
    sections, peers = lax.axis_size("section"), lax.axis_size("dp")
    waves, rows, share = checkpoints.shape[1:]
    quarter = share * peers
    width = 4 * quarter
    hidden = w_in.shape[2]
    half = rows // 2
    odd = lax.axis_index("dp") % 2
    x = checkpoints[0]
    wide = jnp.concatenate([x, x], axis=-1)
    lane = lax.broadcasted_iota(jnp.int32, wide.shape, 2)
    wide = jnp.where(lane // share == odd, wide, jnp.zeros_like(wide))
    vmem = pl.BlockSpec(memory_space=pltpu.VMEM)
    sizes = (waves, rows, width, quarter, hidden, sections, peers)

    def v(shape, kind=BF16):
        return pltpu.VMEM(shape, kind)

    gin, gout, gg, dxo = pl.pallas_call(
        functools.partial(chain, sizes),
        out_shape=(
            jax.ShapeDtypeStruct((quarter, hidden), BF16),
            jax.ShapeDtypeStruct((hidden, quarter), BF16),
            jax.ShapeDtypeStruct((8, 128), F32),
            jax.ShapeDtypeStruct((waves, rows, 128), BF16),
        ),
        in_specs=[vmem] * 5,
        out_specs=(vmem,) * 4,
        scratch_shapes=[
            v((waves, rows, 128)), v((waves, rows, 128)), v((waves, rows, quarter)),
            v((waves, rows, quarter)), v((waves, half, 128)), v((waves, peers, half, 128)),
            v((waves, rows, quarter)), v((waves, half, 128)), v((waves, half, 128)),
            v((waves, rows, hidden + 128)), v((waves, rows, hidden + 128)),
            v((waves, rows, hidden + 128)), v((waves, rows, hidden + 128)),
            v((waves, rows, hidden), F32), v((waves, rows, 128), F32),
            v((waves, rows, hidden), F32), v((waves, rows, hidden), F32),
            v((waves, rows, hidden)), v((waves, rows, hidden)), v((waves, rows, quarter)),
            v((waves, rows, 128), F32),
            v((waves, rows, hidden)), v((waves, rows, hidden)),
            v((waves, rows, hidden)), v((waves, rows, hidden)),
            v((waves, rows, hidden), F32), v((8, quarter), F32), v((peers, 8, 128), F32),
            pltpu.SemaphoreType.DMA((7,)), pltpu.SemaphoreType.DMA((16, waves)),
        ],
        compiler_params=pltpu.CompilerParams(collective_id=0, has_side_effects=True),
        name="chain",
    )(wide, cotangent, gain, w_in[0], w_out[0])
    start = odd * share
    mine = lax.dynamic_slice_in_dim(dxo, start, share, 2)
    gain_share = lax.dynamic_slice_in_dim(gg[:1], start, share, 1)
    return gin[None], gout[None], gain_share, mine[None]


def solution(mesh):
    in_specs = (
        P("section", None, None, "dp"),
        P("section", None),
        P("section", None, "dp"),
        P("section", "dp", None),
        P(None, None, "dp"),
    )
    out_specs = (
        P("section", None, "dp"),
        P("section", "dp", None),
        P("section", "dp"),
        P("section", None, None, "dp"),
    )
    return jax.shard_map(shards, mesh=mesh, in_specs=in_specs, out_specs=out_specs, check_vma=False)
```

```python
import functools

import jax
import jax.numpy as jnp
from jax import lax
from jax.experimental import pallas as pl
from jax.experimental.pallas import tpu as pltpu
from jax.sharding import PartitionSpec as P

MESH = pl.DeviceIdType.MESH
F32 = jnp.float32
BF16 = jnp.bfloat16
K0 = 0.7978845608028654
K1 = 0.044715
SUB = 4
AT_P1, AT_P2, AT_P3 = 1, 3, 5
AT_A, AT_B1, AT_B2, AT_E = 2, 3, 5, 7


def dot_nn(a, b):
    return lax.dot_general(a, b, (((1,), (0,)), ((), ())), preferred_element_type=F32)


def dot_nt(a, b):
    return lax.dot_general(a, b, (((1,), (1,)), ((), ())), preferred_element_type=F32)


def dot_tn(a, b):
    return lax.dot_general(a, b, (((0,), (0,)), ((), ())), preferred_element_type=F32)


def chain(
    sizes,
    x_ref, cot_ref, gain_ref, win_hbm, wout_hbm,
    hid, dact, ub, dy, gg_ref, dxo_ref,
    win_ref, wout_ref,
    xsib, xs, xg, shin, rs, qs, dxs, dxsib,
    a1s, a1r, a2s, a2r, apart, sqs, act, slope, rb,
    d1s, d1r, d2s, d2r, dpart, ggacc, ggr,
    sem1, semw,
):
    waves, rows, width, quarter, hidden, sections, peers = sizes
    half = rows // 2
    s = lax.axis_index("section")
    d = lax.axis_index("dp")
    layer, j = s // 4, s % 4
    top = sections // 4 - 1
    g, c = d // 2, d % 2
    sib = d + 1 - 2 * c
    near = s + 1 - 2 * (s % 2)
    far = s + 2 - 4 * ((s // 2) % 2)
    below = (s + sections - 4) % sections
    above = (s + 4) % sections

    SX, RX, SC, SG, RG, LI, LO = range(7)
    (S_XG, R_XG, S_A1, R_A1, S_A2, R_A2, S_SH, R_SH, S_DY, R_DY,
     S_D1, R_D1, S_D2, R_D2, S_RS, R_RS, S_SP, R_SP) = range(18)

    def at(section, dp):
        return {"section": section, "dp": dp}

    def remote(src, dst, send, recv, section, dp):
        return pltpu.make_async_remote_copy(
            src_ref=src, dst_ref=dst, send_sem=send, recv_sem=recv,
            device_id=at(section, dp), device_id_type=MESH,
        )

    def take(ref, sem):
        pltpu.make_async_copy(ref, ref, sem).wait()

    load_in = pltpu.make_async_copy(win_hbm, win_ref, sem1.at[LI])
    load_out = pltpu.make_async_copy(wout_hbm, wout_ref, sem1.at[LO])
    load_in.start()
    load_out.start()

    barrier = pltpu.get_barrier_semaphore()
    for k in range(1, peers):
        pl.semaphore_signal(barrier, inc=1, device_id=at(s, (d + k) % peers), device_id_type=MESH)
    for other in (near, far, below, above):
        pl.semaphore_signal(barrier, inc=1, device_id=at(other, d), device_id_type=MESH)
    pl.semaphore_wait(barrier, peers + 3)

    own_rows = pl.ds(pl.multiple_of(c * half, half), half)
    other_rows = pl.ds(pl.multiple_of((1 - c) * half, half), half)
    own_cols = pl.ds(pl.multiple_of(g * 128, 128), 128)

    pair = remote(x_ref, xsib, sem1.at[SX], sem1.at[RX], s, sib)
    pair.start()

    per = width // quarter
    q = d % per
    holds_cot = (layer == top) & (d // per == j)

    def cot_copies(w, start):
        for b in range(2):
            for hf in range(2):
                owner = q * 4 + b * 2 + hf
                src = cot_ref.at[w, pl.ds(hf * half, half), pl.ds(b * 128, 128)]
                dst = shin.at[w]

                if start:
                    @pl.when(owner == d)
                    def _():
                        pltpu.make_async_copy(src, dst, semw.at[R_SH, w]).start()

                @pl.when(owner != d)
                def _():
                    copy = remote(src, dst, sem1.at[SC], semw.at[R_SH, w], s, owner)
                    if start:
                        copy.start()
                    else:
                        copy.wait_send()

    @pl.when(holds_cot)
    def _():
        @pl.loop(0, waves)
        def _(w):
            cot_copies(w, True)

    def to_everyone(src, buf, send, recv, w):
        dst = buf.at[w, own_rows, own_cols]
        for k in range(1, peers):
            remote(src, dst, semw.at[send, w], semw.at[recv, w], s, (d + k) % peers).start()
        pltpu.make_async_copy(src, dst, semw.at[recv, w]).start()

    pair.wait_recv()

    @pl.loop(0, waves)
    def _(w):
        xs[w] = x_ref[w] + xsib[w]
        to_everyone(xs.at[w, own_rows], xg, S_XG, R_XG, w)

    ggacc[...] = jnp.zeros_like(ggacc)
    load_in.wait()
    load_out.wait()

    def stage_p1(w):
        take(xg.at[w], semw.at[R_XG, w])
        gain = gain_ref[...]
        xf = xg[w].astype(F32)
        sq = jnp.sum(xf * xf, axis=-1, keepdims=True)
        sq = jnp.broadcast_to(sq, (rows, 128))
        part = dot_nn((xf * gain).astype(BF16), win_ref[...])
        apart[w] = part
        sqs[w] = sq
        a1s[w, :, :hidden] = part.astype(BF16)
        a1s[w, :, hidden:] = sq.astype(BF16)
        remote(a1s.at[w], a1r.at[w], semw.at[S_A1, w], semw.at[R_A1, w], near, d).start()

    def stage_p2(w):
        take(a1r.at[w], semw.at[R_A1, w])
        part = apart[w] + a1r[w, :, :hidden].astype(F32)
        sq = sqs[w] + a1r[w, :, hidden:].astype(F32)
        apart[w] = part
        sqs[w] = sq
        a2s[w, :, :hidden] = part.astype(BF16)
        a2s[w, :, hidden:] = sq.astype(BF16)
        remote(a2s.at[w], a2r.at[w], semw.at[S_A2, w], semw.at[R_A2, w], far, d).start()

    def stage_p3(w):
        take(a2r.at[w], semw.at[R_A2, w])
        gain = gain_ref[...]
        part = apart[w] + a2r[w, :, :hidden].astype(F32)
        sq = sqs[w] + a2r[w, :, hidden:].astype(F32)
        r = lax.rsqrt(sq / width + 1e-06)
        rb[w] = r
        r1 = r[:, :1]
        a = part * r1
        t = jnp.tanh(K0 * (a + K1 * a * a * a))
        act[w] = a
        hid[w] = (0.5 * a * (1.0 + t)).astype(BF16)
        slope[w] = 0.5 * (1.0 + t) + 0.5 * a * (1.0 - t * t) * (K0 * (1.0 + 3.0 * K1 * a * a))
        ub[w] = (xg[w].astype(F32) * r1 * gain).astype(BF16)

    def stage_g(w):
        take(shin.at[w], semw.at[R_SH, w])
        to_everyone(shin.at[w], dy, S_DY, R_DY, w)

    def stage_a(w):
        take(dy.at[w], semw.at[R_DY, w])
        part = dot_nt(dy[w], wout_ref[...])
        dpart[w] = part
        d1s[w] = part.astype(BF16)
        remote(d1s.at[w], d1r.at[w], semw.at[S_D1, w], semw.at[R_D1, w], near, d).start()

    def stage_b1(w):
        take(d1r.at[w], semw.at[R_D1, w])
        part = dpart[w] + d1r[w].astype(F32)
        dpart[w] = part
        d2s[w] = part.astype(BF16)
        remote(d2s.at[w], d2r.at[w], semw.at[S_D2, w], semw.at[R_D2, w], far, d).start()

    def stage_b2(w):
        take(d2r.at[w], semw.at[R_D2, w])
        gain = gain_ref[...]
        dh = dpart[w] + d2r[w].astype(F32)
        da = (slope[w] * dh).astype(BF16)
        dact[w] = da
        r1 = rb[w, :, :1]
        mean = jnp.sum(da.astype(F32) * act[w], axis=-1, keepdims=True) / width
        p = dot_nt(da, win_ref[...])
        n = xg[w].astype(F32) * r1
        qs[w] = ((p * gain - n * mean) * r1).astype(BF16)
        for k in range(1, peers):
            e = (d + k) % peers
            src = qs.at[w, pl.ds(pl.multiple_of(e % 2 * half, half), half),
                        pl.ds(pl.multiple_of(e // 2 * 128, 128), 128)]
            remote(src, rs.at[w, k], semw.at[S_RS, w], semw.at[R_RS, w], s, e).start()
        pltpu.make_async_copy(qs.at[w, own_rows, own_cols], rs.at[w, 0], semw.at[R_RS, w]).start()
        ggacc[...] += jnp.broadcast_to(jnp.sum(p * n, axis=0, keepdims=True), ggacc.shape)

        @pl.when(w == waves - 1)
        def _():
            for k in range(1, peers):
                e = (d + k) % peers
                src = ggacc.at[:, pl.ds(pl.multiple_of(e // 2 * 128, 128), 128)]
                remote(src, ggr.at[k], sem1.at[SG], sem1.at[RG], s, e).start()
            pltpu.make_async_copy(ggacc.at[:, own_cols], ggr.at[0], sem1.at[RG]).start()

    def stage_e(w):
        take(rs.at[w], semw.at[R_RS, w])
        total = dy[w, own_rows, own_cols].astype(F32)
        for k in range(peers):
            total = total + rs[w, k].astype(F32)
        total = total.astype(BF16)
        dxs[w] = total

        @pl.when(layer > 0)
        def _():
            remote(dxs.at[w], shin.at[w], semw.at[S_SH, w], semw.at[R_SH, w], below, d).start()

        remote(dxs.at[w], dxsib.at[w], semw.at[S_SP, w], semw.at[R_SP, w], s, sib).start()
        dxo_ref[w, own_rows, :] = total

    lag = jnp.where(layer == top, 0, waves + AT_P3 + 1)
    steps = waves + AT_E + waves + AT_P3 + 1

    @pl.loop(0, steps)
    def _(t):
        for w, stage in (
            (t - lag, stage_g),
            (t - AT_P2, stage_p2),
            (t - AT_P3, stage_p3),
            (t - AT_A - lag, stage_a),
            (t - AT_B1 - lag, stage_b1),
            (t - AT_B2 - lag, stage_b2),
            (t - AT_E - lag, stage_e),
            (t - AT_P1, stage_p1),
        ):
            pl.when((w >= 0) & (w < waves))(functools.partial(stage, w))

    take(ggr, sem1.at[RG])
    gg = ggr[0]
    for k in range(1, peers):
        gg = gg + ggr[k]
    gg_ref[...] = gg

    pair.wait_send()
    take(ggr.at[pl.ds(1, peers - 1)], sem1.at[SG])

    @pl.when(holds_cot)
    def _():
        @pl.loop(0, waves)
        def _(w):
            cot_copies(w, False)

    @pl.loop(0, waves)
    def _(w):
        take(dxsib.at[w], semw.at[R_SP, w])
        dxo_ref[w, other_rows, :] = dxsib[w]
        for send in (S_XG, S_DY, S_RS):
            take(rs.at[w, pl.ds(1, peers - 1)], semw.at[send, w])
        take(a1s.at[w], semw.at[S_A1, w])
        take(a2s.at[w], semw.at[S_A2, w])
        take(d1s.at[w], semw.at[S_D1, w])
        take(d2s.at[w], semw.at[S_D2, w])
        take(dxs.at[w], semw.at[S_SP, w])

        @pl.when(layer > 0)
        def _():
            take(dxs.at[w], semw.at[S_SH, w])


def weight_grads(share, hid, dact, ub, dy, gg_ref, dxo_ref, gin_ref, gout_ref, gain_ref, mine_ref):
    gout_ref[...] = dot_tn(hid[...], dy[...]).astype(BF16)
    gin_ref[...] = dot_tn(ub[...], dact[...]).astype(BF16)
    odd = lax.axis_index("dp") % 2

    @pl.when(odd == 0)
    def _():
        gain_ref[...] = gg_ref[:1, :share]
        mine_ref[...] = dxo_ref[:, :share]

    @pl.when(odd == 1)
    def _():
        gain_ref[...] = gg_ref[:1, share:]
        mine_ref[...] = dxo_ref[:, share:]


def shards(checkpoints, gain, w_in, w_out, cotangent):
    sections, peers = lax.axis_size("section"), lax.axis_size("dp")
    waves, rows, share = checkpoints.shape[1:]
    tokens = waves * rows
    waves, rows = waves * SUB, rows // SUB
    quarter = share * peers
    width = 4 * quarter
    hidden = w_in.shape[2]
    half = rows // 2
    odd = lax.axis_index("dp") % 2
    x = checkpoints[0].reshape(waves, rows, share)
    wide = jnp.concatenate([x, x], axis=-1)
    lane = lax.broadcasted_iota(jnp.int32, wide.shape, 2)
    wide = jnp.where(lane // share == odd, wide, jnp.zeros_like(wide))
    vmem = pl.BlockSpec(memory_space=pltpu.VMEM)
    anywhere = pl.BlockSpec(memory_space=pl.ANY)
    sizes = (waves, rows, width, quarter, hidden, sections, peers)

    def v(shape, kind=BF16):
        return pltpu.VMEM(shape, kind)

    def o(shape, kind=BF16):
        return jax.ShapeDtypeStruct(shape, kind)

    hid, dact, ub, dy, gg, dxo = pl.pallas_call(
        functools.partial(chain, sizes),
        out_shape=(
            o((waves, rows, hidden)), o((waves, rows, hidden)),
            o((waves, rows, quarter)), o((waves, rows, quarter)),
            o((8, 128), F32), o((waves, rows, 128)),
        ),
        in_specs=[vmem] * 3 + [anywhere] * 2,
        out_specs=(vmem,) * 6,
        scratch_shapes=[
            v((quarter, hidden)), v((hidden, quarter)),
            v((waves, rows, 128)), v((waves, rows, 128)), v((waves, rows, quarter)),
            v((waves, half, 128)), v((waves, peers, half, 128)),
            v((waves, rows, quarter)), v((waves, half, 128)), v((waves, half, 128)),
            v((waves, rows, hidden + 128)), v((waves, rows, hidden + 128)),
            v((waves, rows, hidden + 128)), v((waves, rows, hidden + 128)),
            v((waves, rows, hidden), F32), v((waves, rows, 128), F32),
            v((waves, rows, hidden), F32), v((waves, rows, hidden), F32),
            v((waves, rows, 128), F32),
            v((waves, rows, hidden)), v((waves, rows, hidden)),
            v((waves, rows, hidden)), v((waves, rows, hidden)),
            v((waves, rows, hidden), F32), v((8, quarter), F32), v((peers, 8, 128), F32),
            pltpu.SemaphoreType.DMA((7,)), pltpu.SemaphoreType.DMA((18, waves)),
        ],
        compiler_params=pltpu.CompilerParams(collective_id=0, has_side_effects=True),
        name="chain",
    )(wide, cotangent.reshape(waves, rows, -1), gain, w_in[0], w_out[0])
    gin, gout, gain_share, mine = pl.pallas_call(
        functools.partial(weight_grads, share),
        out_shape=(o((quarter, hidden)), o((hidden, quarter)), o((1, share), F32), o((tokens, share))),
        in_specs=[vmem] * 6,
        out_specs=(vmem,) * 4,
        name="weight_grads",
    )(
        hid.reshape(tokens, hidden), dact.reshape(tokens, hidden),
        ub.reshape(tokens, quarter), dy.reshape(tokens, quarter), gg, dxo.reshape(tokens, 128),
    )
    return gin[None], gout[None], gain_share, mine.reshape(checkpoints.shape)


def solution(mesh):
    in_specs = (
        P("section", None, None, "dp"),
        P("section", None),
        P("section", None, "dp"),
        P("section", "dp", None),
        P(None, None, "dp"),
    )
    out_specs = (
        P("section", None, "dp"),
        P("section", "dp", None),
        P("section", "dp"),
        P("section", None, None, "dp"),
    )
    return jax.shard_map(shards, mesh=mesh, in_specs=in_specs, out_specs=out_specs, check_vma=False)
```

```python
import functools

import jax
import jax.numpy as jnp
from jax import lax
from jax.experimental import pallas as pl
from jax.experimental.pallas import tpu as pltpu
from jax.sharding import PartitionSpec as P

MESH = pl.DeviceIdType.MESH
F32 = jnp.float32
BF16 = jnp.bfloat16
K0 = 0.7978845608028654
K1 = 0.044715
SUB = 4
GRID = 4
P1, P2, P3 = 1, 5, 11
A, B1, B2, E = (6, 2), (8, 3), (11, 6), (14, 9)
LAG = 0
ORDER = ('P3', 'G', 'P2', 'E', 'B2', 'P1', 'A', 'B1')
FAR_FIRST = (8, 7, 9, 6, 10, 5, 11, 4, 12, 3, 13, 2, 14, 1, 15)


def dot_nn(a, b):
    return lax.dot_general(a, b, (((1,), (0,)), ((), ())), preferred_element_type=F32)


def dot_tn(a, b):
    return lax.dot_general(a, b, (((0,), (0,)), ((), ())), preferred_element_type=F32)


def chain(
    sizes,
    x_in, cot_ref, gain_ref, win_hbm, wout_hbm,
    hid, dact, ub, dy, gg_ref, dxo_ref,
    win_ref, wout_ref, win_t, wout_t, x_ref,
    xsib, xs, xg, shin, rs, qs, dxs, dxsib,
    a1s, a1r, a2s, a2r, apart, sqs, act, slope, rb,
    d1s, d1r, d2s, d2r, dpart, ggacc, ggr, zr,
    sem1, semw,
):
    waves, rows, width, quarter, hidden, sections, peers = sizes
    half = rows // 2
    s = lax.axis_index("section")
    d = lax.axis_index("dp")
    layer, j = s // 4, s % 4
    top = sections // 4 - 1
    is_top = layer == top
    g, c = d // 2, d % 2
    sib = d + 1 - 2 * c
    near = s + 1 - 2 * (s % 2)
    far = s + 2 - 4 * ((s // 2) % 2)
    below = (s + sections - 4) % sections
    above = (s + 4) % sections

    SX, RX, SC, SG, RG, LI, LO = range(7)
    (S_XG, R_XG, S_A1, R_A1, S_A2, R_A2, S_SH, R_SH, S_DY, R_DY,
     S_D1, R_D1, S_D2, R_D2, S_RS, R_RS, S_SP, R_SP, S_Z, R_Z) = range(20)

    def at(section, dp):
        return {"section": section, "dp": dp}

    def remote(src, dst, send, recv, section, dp):
        return pltpu.make_async_remote_copy(
            src_ref=src, dst_ref=dst, send_sem=send, recv_sem=recv,
            device_id=at(section, dp), device_id_type=MESH,
        )

    def take(ref, sem):
        pltpu.make_async_copy(ref, ref, sem).wait()

    load_in = pltpu.make_async_copy(win_hbm, win_ref, sem1.at[LI])
    load_out = pltpu.make_async_copy(wout_hbm, wout_ref, sem1.at[LO])
    load_in.start()
    load_out.start()

    share = x_in.shape[2]
    wide = jnp.concatenate([x_in[...], x_in[...]], axis=-1)
    lane = lax.broadcasted_iota(jnp.int32, wide.shape, 2)
    x_ref[...] = jnp.where((lane >= share) == (c == 1), wide, jnp.zeros_like(wide))

    barrier = pltpu.get_barrier_semaphore()
    for k in range(1, peers):
        pl.semaphore_signal(barrier, inc=1, device_id=at(s, (d + k) % peers), device_id_type=MESH)
    for other in (near, far, s - j + 3 - j, below, above):
        pl.semaphore_signal(barrier, inc=1, device_id=at(other, d), device_id_type=MESH)
    pl.semaphore_wait(barrier, peers + 4)

    own_rows = pl.ds(pl.multiple_of(c * half, half), half)
    other_rows = pl.ds(pl.multiple_of((1 - c) * half, half), half)
    own_cols = pl.ds(pl.multiple_of(g * 128, 128), 128)

    pair = remote(x_ref, xsib, sem1.at[SX], sem1.at[RX], s, sib)
    pair.start()

    per = width // quarter
    q = d % per
    holds_cot = (layer == top) & (d // per == j)

    def cot_copies(w, start):
        for b in range(2):
            for hf in range(2):
                owner = q * 4 + b * 2 + hf
                src = cot_ref.at[w, pl.ds(hf * half, half), pl.ds(b * 128, 128)]
                dst = shin.at[w]

                if start:
                    @pl.when(owner == d)
                    def _():
                        pltpu.make_async_copy(src, dst, semw.at[R_SH, w]).start()

                @pl.when(owner != d)
                def _():
                    copy = remote(src, dst, sem1.at[SC], semw.at[R_SH, w], s, owner)
                    if start:
                        copy.start()
                    else:
                        copy.wait_send()

    @pl.when(holds_cot)
    def _():
        @pl.loop(0, waves)
        def _(w):
            cot_copies(w, True)

    def to_everyone(src, buf, send, recv, w):
        dst = buf.at[w, own_rows, own_cols]
        for k in FAR_FIRST:
            remote(src, dst, semw.at[send, w], semw.at[recv, w], s, (d + k) % peers).start()
        pltpu.make_async_copy(src, dst, semw.at[recv, w]).start()

    pair.wait_recv()

    @pl.loop(0, waves)
    def _(w):
        xs[w] = x_ref[w] + xsib[w]
        to_everyone(xs.at[w, own_rows], xg, S_XG, R_XG, w)

    ggacc[...] = jnp.zeros_like(ggacc)
    load_in.wait()
    load_out.wait()
    win_t[...] = win_ref[...].T
    wout_t[...] = wout_ref[...].T

    def stage_p1(w):
        take(xg.at[w], semw.at[R_XG, w])
        gain = gain_ref[...]
        xf = xg[w].astype(F32)
        sq = jnp.sum(xf * xf, axis=-1, keepdims=True)
        sq = jnp.broadcast_to(sq, (rows, 128))
        part = dot_nn((xf * gain).astype(BF16), win_ref[...])
        apart[w] = part
        sqs[w] = sq
        a1s[w, :, :hidden] = part.astype(BF16)
        a1s[w, :, hidden:] = sq.astype(BF16)
        remote(a1s.at[w], a1r.at[w], semw.at[S_A1, w], semw.at[R_A1, w], near, d).start()

    def stage_p2(w):
        take(a1r.at[w], semw.at[R_A1, w])
        part = apart[w] + a1r[w, :, :hidden].astype(F32)
        sq = sqs[w] + a1r[w, :, hidden:].astype(F32)
        apart[w] = part
        sqs[w] = sq
        a2s[w, :, :hidden] = part.astype(BF16)
        a2s[w, :, hidden:] = sq.astype(BF16)
        remote(a2s.at[w], a2r.at[w], semw.at[S_A2, w], semw.at[R_A2, w], far, d).start()

    def stage_p3(w):
        take(a2r.at[w], semw.at[R_A2, w])
        gain = gain_ref[...]
        part = apart[w] + a2r[w, :, :hidden].astype(F32)
        sq = sqs[w] + a2r[w, :, hidden:].astype(F32)
        r = lax.rsqrt(sq / width + 1e-06)
        rb[w] = r
        r1 = r[:, :1]
        a = part * r1
        t = jnp.tanh(K0 * (a + K1 * a * a * a))
        act[w] = a
        hid[w] = (0.5 * a * (1.0 + t)).astype(BF16)
        slope[w] = 0.5 * (1.0 + t) + 0.5 * a * (1.0 - t * t) * (K0 * (1.0 + 3.0 * K1 * a * a))
        ub[w] = (xg[w].astype(F32) * r1 * gain).astype(BF16)

    def stage_g(w):
        take(shin.at[w], semw.at[R_SH, w])
        to_everyone(shin.at[w], dy, S_DY, R_DY, w)

    def stage_a(w):
        take(dy.at[w], semw.at[R_DY, w])
        part = dot_nn(dy[w], wout_t[...])
        dpart[w] = part
        d1s[w] = part.astype(BF16)

        @pl.when(is_top)
        def _():
            remote(d1s.at[w], d1r.at[w], semw.at[S_D1, w], semw.at[R_D1, w], near, d).start()

        @pl.when(layer != top)
        def _():
            for k in (2, 1, 3):
                other = s - j + (j + k) % 4
                remote(d1s.at[w], zr.at[w, k - 1], semw.at[S_Z, w], semw.at[R_Z, w], other, d).start()

    def stage_b1(w):
        take(d1r.at[w], semw.at[R_D1, w])
        part = dpart[w] + d1r[w].astype(F32)
        dpart[w] = part
        d2s[w] = part.astype(BF16)
        remote(d2s.at[w], d2r.at[w], semw.at[S_D2, w], semw.at[R_D2, w], far, d).start()

    def stage_b2(w):
        @pl.when(is_top)
        def _():
            take(d2r.at[w], semw.at[R_D2, w])
            dpart[w] = dpart[w] + d2r[w].astype(F32)

        @pl.when(layer != top)
        def _():
            take(zr.at[w], semw.at[R_Z, w])
            dpart[w] = dpart[w] + zr[w, 0].astype(F32) + zr[w, 1].astype(F32) + zr[w, 2].astype(F32)

        gain = gain_ref[...]
        dh = dpart[w]
        da = (slope[w] * dh).astype(BF16)
        dact[w] = da
        r1 = rb[w, :, :1]
        mean = jnp.sum(da.astype(F32) * act[w], axis=-1, keepdims=True) / width
        p = dot_nn(da, win_t[...])
        n = xg[w].astype(F32) * r1
        qs[w] = ((p * gain - n * mean) * r1).astype(BF16)
        for k in FAR_FIRST:
            e = (d + k) % peers
            src = qs.at[w, pl.ds(pl.multiple_of(e % 2 * half, half), half),
                        pl.ds(pl.multiple_of(e // 2 * 128, 128), 128)]
            remote(src, rs.at[w, k], semw.at[S_RS, w], semw.at[R_RS, w], s, e).start()
        pltpu.make_async_copy(qs.at[w, own_rows, own_cols], rs.at[w, 0], semw.at[R_RS, w]).start()
        ggacc[...] += jnp.sum((p * n).reshape(rows // 8, 8, quarter), axis=0)

        @pl.when(w == waves - 1)
        def _():
            for k in range(1, peers):
                e = (d + k) % peers
                src = ggacc.at[:, pl.ds(pl.multiple_of(e // 2 * 128, 128), 128)]
                remote(src, ggr.at[k], sem1.at[SG], sem1.at[RG], s, e).start()
            pltpu.make_async_copy(ggacc.at[:, own_cols], ggr.at[0], sem1.at[RG]).start()

    def stage_e(w):
        take(rs.at[w], semw.at[R_RS, w])
        total = dy[w, own_rows, own_cols].astype(F32)
        for k in range(peers):
            total = total + rs[w, k].astype(F32)
        total = total.astype(BF16)
        dxs[w] = total

        @pl.when(layer > 0)
        def _():
            remote(dxs.at[w], shin.at[w], semw.at[S_SH, w], semw.at[R_SH, w], below, d).start()

        remote(dxs.at[w], dxsib.at[w], semw.at[S_SP, w], semw.at[R_SP, w], s, sib).start()
        dxo_ref[w, own_rows, :] = total

    base = jnp.where(is_top, LAG, waves + P3 + 1)
    steps = waves + max(LAG + E[0], waves + P3 + 1 + E[1])

    def chain_at(pair):
        return base + jnp.where(is_top, pair[0], pair[1])

    stages = dict(
        G=(base, stage_g), A=(chain_at(A), stage_a), B1=(chain_at(B1), stage_b1),
        B2=(chain_at(B2), stage_b2), E=(chain_at(E), stage_e),
        P1=(P1, stage_p1), P2=(P2, stage_p2), P3=(P3, stage_p3),
    )

    @pl.loop(0, steps)
    def _(t):
        for start, stage in [stages[name] for name in ORDER]:
            w = t - start
            live = (w >= 0) & (w < waves)
            if stage is stage_b1:
                live = live & is_top
            pl.when(live)(functools.partial(stage, w))

    take(ggr, sem1.at[RG])
    gg = ggr[0]
    for k in range(1, peers):
        gg = gg + ggr[k]
    gg_ref[...] = gg

    pair.wait_send()
    take(ggr.at[pl.ds(1, peers - 1)], sem1.at[SG])

    @pl.when(holds_cot)
    def _():
        @pl.loop(0, waves)
        def _(w):
            cot_copies(w, False)

    @pl.loop(0, waves)
    def _(w):
        take(dxsib.at[w], semw.at[R_SP, w])
        dxo_ref[w, other_rows, :] = dxsib[w]
        for send in (S_XG, S_DY, S_RS):
            take(rs.at[w, pl.ds(1, peers - 1)], semw.at[send, w])
        take(a1s.at[w], semw.at[S_A1, w])
        take(a2s.at[w], semw.at[S_A2, w])

        @pl.when(is_top)
        def _():
            take(d1s.at[w], semw.at[S_D1, w])
            take(d2s.at[w], semw.at[S_D2, w])

        @pl.when(layer != top)
        def _():
            take(zr.at[w], semw.at[S_Z, w])

        take(dxs.at[w], semw.at[S_SP, w])

        @pl.when(layer > 0)
        def _():
            take(dxs.at[w], semw.at[S_SH, w])


def weight_grads(share, hid, dact, ub, dy, gg_ref, dxo_ref, gin_ref, gout_ref, gain_ref, mine_ref):
    gout_ref[...] = dot_tn(hid[...], dy[...]).astype(BF16)
    gin_ref[...] = dot_tn(ub[...], dact[...]).astype(BF16)
    odd = lax.axis_index("dp") % 2
    first = pl.program_id(0) == 0

    @pl.when(first & (odd == 0))
    def _():
        gain_ref[...] = jnp.sum(gg_ref[:, :share], axis=0, keepdims=True)
        mine_ref[...] = dxo_ref[:, :share]

    @pl.when(first & (odd == 1))
    def _():
        gain_ref[...] = jnp.sum(gg_ref[:, share:], axis=0, keepdims=True)
        mine_ref[...] = dxo_ref[:, share:]


def shards(checkpoints, gain, w_in, w_out, cotangent):
    sections, peers = lax.axis_size("section"), lax.axis_size("dp")
    waves, rows, share = checkpoints.shape[1:]
    tokens = waves * rows
    waves, rows = waves * SUB, rows // SUB
    quarter = share * peers
    width = 4 * quarter
    hidden = w_in.shape[2]
    half = rows // 2
    x = checkpoints[0].reshape(waves, rows, share)
    vmem = pl.BlockSpec(memory_space=pltpu.VMEM)
    anywhere = pl.BlockSpec(memory_space=pl.ANY)
    sizes = (waves, rows, width, quarter, hidden, sections, peers)

    def whole(*shape):
        return pl.BlockSpec(shape, lambda i: (0, 0))

    def v(shape, kind=BF16):
        return pltpu.VMEM(shape, kind)

    def o(shape, kind=BF16):
        return jax.ShapeDtypeStruct(shape, kind)

    hid, dact, ub, dy, gg, dxo = pl.pallas_call(
        functools.partial(chain, sizes),
        out_shape=(
            o((waves, rows, hidden)), o((waves, rows, hidden)),
            o((waves, rows, quarter)), o((waves, rows, quarter)),
            o((8, 128), F32), o((waves, rows, 128)),
        ),
        in_specs=[vmem] * 3 + [anywhere] * 2,
        out_specs=(vmem,) * 6,
        scratch_shapes=[
            v((quarter, hidden)), v((hidden, quarter)), v((hidden, quarter)), v((quarter, hidden)),
            v((waves, rows, 128)),
            v((waves, rows, 128)), v((waves, rows, 128)), v((waves, rows, quarter)),
            v((waves, half, 128)), v((waves, peers, half, 128)),
            v((waves, rows, quarter)), v((waves, half, 128)), v((waves, half, 128)),
            v((waves, rows, hidden + 128)), v((waves, rows, hidden + 128)),
            v((waves, rows, hidden + 128)), v((waves, rows, hidden + 128)),
            v((waves, rows, hidden), F32), v((waves, rows, 128), F32),
            v((waves, rows, hidden), F32), v((waves, rows, hidden), F32),
            v((waves, rows, 128), F32),
            v((waves, rows, hidden)), v((waves, rows, hidden)),
            v((waves, rows, hidden)), v((waves, rows, hidden)),
            v((waves, rows, hidden), F32), v((8, quarter), F32), v((peers, 8, 128), F32),
            v((waves, 3, rows, hidden)),
            pltpu.SemaphoreType.DMA((7,)), pltpu.SemaphoreType.DMA((20, waves)),
        ],
        compiler_params=pltpu.CompilerParams(collective_id=0, has_side_effects=True),
        name="chain",
    )(x, cotangent.reshape(waves, rows, -1), gain, w_in[0], w_out[0])
    gin, gout, gain_share, mine = pl.pallas_call(
        functools.partial(weight_grads, share),
        out_shape=(o((quarter, hidden)), o((hidden, quarter)), o((1, share), F32), o((tokens, share))),
        grid=(GRID,),
        in_specs=[
            pl.BlockSpec((tokens, hidden // GRID), lambda i: (0, i)), whole(tokens, hidden),
            pl.BlockSpec((tokens, quarter // GRID), lambda i: (0, i)), whole(tokens, quarter),
            whole(8, 128), whole(tokens, 128),
        ],
        out_specs=(
            pl.BlockSpec((quarter // GRID, hidden), lambda i: (i, 0)),
            pl.BlockSpec((hidden // GRID, quarter), lambda i: (i, 0)),
            whole(1, share), whole(tokens, share),
        ),
        name="weight_grads",
    )(
        hid.reshape(tokens, hidden), dact.reshape(tokens, hidden),
        ub.reshape(tokens, quarter), dy.reshape(tokens, quarter), gg, dxo.reshape(tokens, 128),
    )
    return gin[None], gout[None], gain_share, mine.reshape(checkpoints.shape)


def solution(mesh):
    in_specs = (
        P("section", None, None, "dp"),
        P("section", None),
        P("section", None, "dp"),
        P("section", "dp", None),
        P(None, None, "dp"),
    )
    out_specs = (
        P("section", None, "dp"),
        P("section", "dp", None),
        P("section", "dp"),
        P("section", None, None, "dp"),
    )
    return jax.shard_map(shards, mesh=mesh, in_specs=in_specs, out_specs=out_specs, check_vma=False)
```

```python
import functools

import jax
import jax.numpy as jnp
from jax import lax
from jax.experimental import pallas as pl
from jax.experimental.pallas import tpu as pltpu
from jax.sharding import PartitionSpec as P

MESH = pl.DeviceIdType.MESH
F32 = jnp.float32
BF16 = jnp.bfloat16
K0 = 0.7978845608028654
K1 = 0.044715
SUB = 4
P1, P2, P3 = 0, 3, 8
A, B1, B2, E = (5, 3), (7, 6), (10, 7), (12, 9)
LAG = 0
ORDER = ('B2', 'A', 'B1', 'G', 'P3', 'P2', 'E', 'P1')
FAR_FIRST = (8, 7, 9, 6, 10, 5, 11, 4, 12, 3, 13, 2, 14, 1, 15)


def dot_nn(a, b):
    return lax.dot_general(a, b, (((1,), (0,)), ((), ())), preferred_element_type=F32)


def dot_tn(a, b):
    return lax.dot_general(a, b, (((0,), (0,)), ((), ())), preferred_element_type=F32)


def chain(
    sizes,
    x_in, cot_ref, gain_ref, win_hbm, wout_hbm,
    hid, dact, ub, dy, gg_ref, dxo_ref,
    win_ref, wout_ref, win_t, wout_t, x_ref,
    xsib, xs, xg, shin, rs, qs, dxs, dxsib,
    a1s, a1r, a2s, a2r, apart, sqs, act, slope, rb,
    d1s, d1r, d2s, d2r, dpart, ggacc, ggr, zr,
    sem1, semw,
):
    waves, rows, width, quarter, hidden, sections, peers = sizes
    half = rows // 2
    s = lax.axis_index("section")
    d = lax.axis_index("dp")
    layer, j = s // 4, s % 4
    top = sections // 4 - 1
    is_top = layer == top
    g, c = d // 2, d % 2
    sib = d + 1 - 2 * c
    near = s + 1 - 2 * (s % 2)
    far = s + 2 - 4 * ((s // 2) % 2)
    below = (s + sections - 4) % sections
    above = (s + 4) % sections

    SX, RX, SC, SG, RG, LI, LO = range(7)
    (S_XG, R_XG, S_A1, R_A1, S_A2, R_A2, S_SH, R_SH, S_DY, R_DY,
     S_D1, R_D1, S_D2, R_D2, S_RS, R_RS, S_SP, R_SP, S_Z, R_Z) = range(20)

    def at(section, dp):
        return {"section": section, "dp": dp}

    def remote(src, dst, send, recv, section, dp):
        return pltpu.make_async_remote_copy(
            src_ref=src, dst_ref=dst, send_sem=send, recv_sem=recv,
            device_id=at(section, dp), device_id_type=MESH,
        )

    def take(ref, sem):
        pltpu.make_async_copy(ref, ref, sem).wait()

    load_in = pltpu.make_async_copy(win_hbm, win_ref, sem1.at[LI])
    load_out = pltpu.make_async_copy(wout_hbm, wout_ref, sem1.at[LO])
    load_in.start()
    load_out.start()

    share = x_in.shape[2]
    wide = jnp.concatenate([x_in[...], x_in[...]], axis=-1)
    lane = lax.broadcasted_iota(jnp.int32, wide.shape, 2)
    x_ref[...] = jnp.where((lane >= share) == (c == 1), wide, jnp.zeros_like(wide))

    barrier = pltpu.get_barrier_semaphore()
    for k in range(1, peers):
        pl.semaphore_signal(barrier, inc=1, device_id=at(s, (d + k) % peers), device_id_type=MESH)
    for other in (near, far, s - j + 3 - j, below, above):
        pl.semaphore_signal(barrier, inc=1, device_id=at(other, d), device_id_type=MESH)
    pl.semaphore_wait(barrier, peers + 4)

    own_rows = pl.ds(pl.multiple_of(c * half, half), half)
    other_rows = pl.ds(pl.multiple_of((1 - c) * half, half), half)
    own_cols = pl.ds(pl.multiple_of(g * 128, 128), 128)

    pair = remote(x_ref, xsib, sem1.at[SX], sem1.at[RX], s, sib)
    pair.start()

    per = width // quarter
    q = d % per
    holds_cot = (layer == top) & (d // per == j)

    def cot_copies(w, start):
        for b in range(2):
            for hf in range(2):
                owner = q * 4 + b * 2 + hf
                src = cot_ref.at[w, pl.ds(hf * half, half), pl.ds(b * 128, 128)]
                dst = shin.at[w]

                if start:
                    @pl.when(owner == d)
                    def _():
                        pltpu.make_async_copy(src, dst, semw.at[R_SH, w]).start()

                @pl.when(owner != d)
                def _():
                    copy = remote(src, dst, sem1.at[SC], semw.at[R_SH, w], s, owner)
                    if start:
                        copy.start()
                    else:
                        copy.wait_send()

    @pl.when(holds_cot)
    def _():
        @pl.loop(0, waves)
        def _(w):
            cot_copies(w, True)

    def to_everyone(src, buf, send, recv, w):
        dst = buf.at[w, own_rows, own_cols]
        for k in FAR_FIRST:
            remote(src, dst, semw.at[send, w], semw.at[recv, w], s, (d + k) % peers).start()
        pltpu.make_async_copy(src, dst, semw.at[recv, w]).start()

    pair.wait_recv()

    @pl.loop(0, waves)
    def _(w):
        xs[w] = x_ref[w] + xsib[w]
        to_everyone(xs.at[w, own_rows], xg, S_XG, R_XG, w)

    ggacc[...] = jnp.zeros_like(ggacc)
    load_in.wait()
    load_out.wait()
    win_t[...] = win_ref[...].T
    wout_t[...] = wout_ref[...].T

    def stage_p1(w):
        take(xg.at[w], semw.at[R_XG, w])
        gain = gain_ref[...]
        xf = xg[w].astype(F32)
        sq = jnp.sum(xf * xf, axis=-1, keepdims=True)
        sq = jnp.broadcast_to(sq, (rows, 128))
        part = dot_nn((xf * gain).astype(BF16), win_ref[...])
        apart[w] = part
        sqs[w] = sq
        a1s[w, :, :hidden] = part.astype(BF16)
        a1s[w, :, hidden:] = sq.astype(BF16)
        remote(a1s.at[w], a1r.at[w], semw.at[S_A1, w], semw.at[R_A1, w], near, d).start()

    def stage_p2(w):
        take(a1r.at[w], semw.at[R_A1, w])
        part = apart[w] + a1r[w, :, :hidden].astype(F32)
        sq = sqs[w] + a1r[w, :, hidden:].astype(F32)
        apart[w] = part
        sqs[w] = sq
        a2s[w, :, :hidden] = part.astype(BF16)
        a2s[w, :, hidden:] = sq.astype(BF16)
        remote(a2s.at[w], a2r.at[w], semw.at[S_A2, w], semw.at[R_A2, w], far, d).start()

    def stage_p3(w):
        take(a2r.at[w], semw.at[R_A2, w])
        gain = gain_ref[...]
        part = apart[w] + a2r[w, :, :hidden].astype(F32)
        sq = sqs[w] + a2r[w, :, hidden:].astype(F32)
        r = lax.rsqrt(sq / width + 1e-06)
        rb[w] = r
        r1 = r[:, :1]
        a = part * r1
        t = jnp.tanh(K0 * (a + K1 * a * a * a))
        act[w] = a
        hid[w] = (0.5 * a * (1.0 + t)).astype(BF16)
        slope[w] = 0.5 * (1.0 + t) + 0.5 * a * (1.0 - t * t) * (K0 * (1.0 + 3.0 * K1 * a * a))
        ub[w] = (xg[w].astype(F32) * r1 * gain).astype(BF16)

    def stage_g(w):
        take(shin.at[w], semw.at[R_SH, w])
        to_everyone(shin.at[w], dy, S_DY, R_DY, w)

    def stage_a(w):
        take(dy.at[w], semw.at[R_DY, w])
        part = dot_nn(dy[w], wout_t[...])
        dpart[w] = part
        d1s[w] = part.astype(BF16)

        @pl.when(is_top)
        def _():
            remote(d1s.at[w], d1r.at[w], semw.at[S_D1, w], semw.at[R_D1, w], near, d).start()

        @pl.when(layer != top)
        def _():
            for k in (2, 1, 3):
                other = s - j + (j + k) % 4
                remote(d1s.at[w], zr.at[w, k - 1], semw.at[S_Z, w], semw.at[R_Z, w], other, d).start()

    def stage_b1(w):
        take(d1r.at[w], semw.at[R_D1, w])
        part = dpart[w] + d1r[w].astype(F32)
        dpart[w] = part
        d2s[w] = part.astype(BF16)
        remote(d2s.at[w], d2r.at[w], semw.at[S_D2, w], semw.at[R_D2, w], far, d).start()

    def stage_b2(w):
        @pl.when(is_top)
        def _():
            take(d2r.at[w], semw.at[R_D2, w])
            dpart[w] = dpart[w] + d2r[w].astype(F32)

        @pl.when(layer != top)
        def _():
            take(zr.at[w], semw.at[R_Z, w])
            dpart[w] = dpart[w] + zr[w, 0].astype(F32) + zr[w, 1].astype(F32) + zr[w, 2].astype(F32)

        gain = gain_ref[...]
        dh = dpart[w]
        da = (slope[w] * dh).astype(BF16)
        dact[w] = da
        r1 = rb[w, :, :1]
        mean = jnp.sum(da.astype(F32) * act[w], axis=-1, keepdims=True) / width
        p = dot_nn(da, win_t[...])
        n = xg[w].astype(F32) * r1
        qs[w] = ((p * gain - n * mean) * r1).astype(BF16)
        for k in FAR_FIRST:
            e = (d + k) % peers
            src = qs.at[w, pl.ds(pl.multiple_of(e % 2 * half, half), half),
                        pl.ds(pl.multiple_of(e // 2 * 128, 128), 128)]
            remote(src, rs.at[w, k], semw.at[S_RS, w], semw.at[R_RS, w], s, e).start()
        pltpu.make_async_copy(qs.at[w, own_rows, own_cols], rs.at[w, 0], semw.at[R_RS, w]).start()
        ggacc[...] += jnp.sum((p * n).reshape(rows // 8, 8, quarter), axis=0)

        @pl.when(w == waves - 1)
        def _():
            for k in range(1, peers):
                e = (d + k) % peers
                src = ggacc.at[:, pl.ds(pl.multiple_of(e // 2 * 128, 128), 128)]
                remote(src, ggr.at[k], sem1.at[SG], sem1.at[RG], s, e).start()
            pltpu.make_async_copy(ggacc.at[:, own_cols], ggr.at[0], sem1.at[RG]).start()

    def stage_e(w):
        take(rs.at[w], semw.at[R_RS, w])
        total = dy[w, own_rows, own_cols].astype(F32)
        for k in range(peers):
            total = total + rs[w, k].astype(F32)
        total = total.astype(BF16)
        dxs[w] = total

        @pl.when(layer > 0)
        def _():
            remote(dxs.at[w], shin.at[w], semw.at[S_SH, w], semw.at[R_SH, w], below, d).start()

        remote(dxs.at[w], dxsib.at[w], semw.at[S_SP, w], semw.at[R_SP, w], s, sib).start()
        dxo_ref[w, own_rows, :] = total

    base = jnp.where(is_top, LAG, waves + P3 + 1)
    steps = waves + max(LAG + E[0], waves + P3 + 1 + E[1])

    def chain_at(pair):
        return base + jnp.where(is_top, pair[0], pair[1])

    stages = dict(
        G=(base, stage_g), A=(chain_at(A), stage_a), B1=(chain_at(B1), stage_b1),
        B2=(chain_at(B2), stage_b2), E=(chain_at(E), stage_e),
        P1=(P1, stage_p1), P2=(P2, stage_p2), P3=(P3, stage_p3),
    )

    @pl.loop(0, steps)
    def _(t):
        for start, stage in [stages[name] for name in ORDER]:
            w = t - start
            live = (w >= 0) & (w < waves)
            if stage is stage_b1:
                live = live & is_top
            pl.when(live)(functools.partial(stage, w))

    take(ggr, sem1.at[RG])
    gg = ggr[0]
    for k in range(1, peers):
        gg = gg + ggr[k]
    gg_ref[...] = gg

    pair.wait_send()
    take(ggr.at[pl.ds(1, peers - 1)], sem1.at[SG])

    @pl.when(holds_cot)
    def _():
        @pl.loop(0, waves)
        def _(w):
            cot_copies(w, False)

    @pl.loop(0, waves)
    def _(w):
        take(dxsib.at[w], semw.at[R_SP, w])
        dxo_ref[w, other_rows, :] = dxsib[w]
        for send in (S_XG, S_DY, S_RS):
            take(rs.at[w, pl.ds(1, peers - 1)], semw.at[send, w])
        take(a1s.at[w], semw.at[S_A1, w])
        take(a2s.at[w], semw.at[S_A2, w])

        @pl.when(is_top)
        def _():
            take(d1s.at[w], semw.at[S_D1, w])
            take(d2s.at[w], semw.at[S_D2, w])

        @pl.when(layer != top)
        def _():
            take(zr.at[w], semw.at[S_Z, w])

        take(dxs.at[w], semw.at[S_SP, w])

        @pl.when(layer > 0)
        def _():
            take(dxs.at[w], semw.at[S_SH, w])


def weight_grads(
    share, hid, dact, ub, dy, gg_ref, dxo_ref,
    gin_out, gout_out, gain_ref, mine_ref,
    gin, gout, sem,
):
    tokens = dxo_ref.shape[0] * dxo_ref.shape[1]
    odd = lax.axis_index("dp") % 2

    @pl.when(odd == 0)
    def _():
        gain_ref[...] = jnp.sum(gg_ref[:, :share], axis=0, keepdims=True)
        mine_ref[...] = dxo_ref[:, :, :share].reshape(tokens, share)

    @pl.when(odd == 1)
    def _():
        gain_ref[...] = jnp.sum(gg_ref[:, share:], axis=0, keepdims=True)
        mine_ref[...] = dxo_ref[:, :, share:].reshape(tokens, share)

    stores = []

    def product(left, right, result, out, first):
        part = result.shape[0] // 2
        for n in range(2):
            here = pl.ds(n * part, part)
            lhs = left[:, :, n * part:(n + 1) * part].reshape(tokens, part)
            rhs = right[...].reshape(tokens, right.shape[2])
            result[here, :] = dot_tn(lhs, rhs).astype(BF16)
            stores.append(pltpu.make_async_copy(result.at[here], out.at[here], sem.at[first + n]))
            stores[-1].start()

    product(hid, dy, gout, gout_out, 0)
    product(ub, dact, gin, gin_out, 2)
    for store in stores:
        store.wait()


def shards(checkpoints, gain, w_in, w_out, cotangent):
    sections, peers = lax.axis_size("section"), lax.axis_size("dp")
    waves, rows, share = checkpoints.shape[1:]
    tokens = waves * rows
    waves, rows = waves * SUB, rows // SUB
    quarter = share * peers
    width = 4 * quarter
    hidden = w_in.shape[2]
    half = rows // 2
    x = checkpoints[0].reshape(waves, rows, share)
    vmem = pl.BlockSpec(memory_space=pltpu.VMEM)
    anywhere = pl.BlockSpec(memory_space=pl.ANY)
    sizes = (waves, rows, width, quarter, hidden, sections, peers)

    def v(shape, kind=BF16):
        return pltpu.VMEM(shape, kind)

    def o(shape, kind=BF16):
        return jax.ShapeDtypeStruct(shape, kind)

    hid, dact, ub, dy, gg, dxo = pl.pallas_call(
        functools.partial(chain, sizes),
        out_shape=(
            pltpu.VMEM((waves, rows, hidden), BF16), pltpu.VMEM((waves, rows, hidden), BF16),
            pltpu.VMEM((waves, rows, quarter), BF16), pltpu.VMEM((waves, rows, quarter), BF16),
            pltpu.VMEM((8, 128), F32), pltpu.VMEM((waves, rows, 128), BF16),
        ),
        in_specs=[vmem] * 3 + [anywhere] * 2,
        out_specs=(vmem,) * 6,
        scratch_shapes=[
            v((quarter, hidden)), v((hidden, quarter)), v((hidden, quarter)), v((quarter, hidden)),
            v((waves, rows, 128)),
            v((waves, rows, 128)), v((waves, rows, 128)), v((waves, rows, quarter)),
            v((waves, half, 128)), v((waves, peers, half, 128)),
            v((waves, rows, quarter)), v((waves, half, 128)), v((waves, half, 128)),
            v((waves, rows, hidden + 128)), v((waves, rows, hidden + 128)),
            v((waves, rows, hidden + 128)), v((waves, rows, hidden + 128)),
            v((waves, rows, hidden), F32), v((waves, rows, 128), F32),
            v((waves, rows, hidden), F32), v((waves, rows, hidden), F32),
            v((waves, rows, 128), F32),
            v((waves, rows, hidden)), v((waves, rows, hidden)),
            v((waves, rows, hidden)), v((waves, rows, hidden)),
            v((waves, rows, hidden), F32), v((8, quarter), F32), v((peers, 8, 128), F32),
            v((waves, 3, rows, hidden)),
            pltpu.SemaphoreType.DMA((7,)), pltpu.SemaphoreType.DMA((20, waves)),
        ],
        compiler_params=pltpu.CompilerParams(collective_id=0, has_side_effects=True),
        name="chain",
    )(x, cotangent.reshape(waves, rows, -1), gain, w_in[0], w_out[0])
    gin, gout, gain_share, mine = pl.pallas_call(
        functools.partial(weight_grads, share),
        out_shape=(o((quarter, hidden)), o((hidden, quarter)), o((1, share), F32), o((tokens, share))),
        in_specs=[vmem] * 6,
        out_specs=(anywhere, anywhere, vmem, vmem),
        scratch_shapes=[
            v((quarter, hidden)), v((hidden, quarter)), pltpu.SemaphoreType.DMA((4,)),
        ],
        name="weight_grads",
    )(
        *[pltpu.with_memory_space_constraint(a, pltpu.MemorySpace.VMEM) for a in (hid, dact, ub, dy, gg, dxo)],
    )
    return gin[None], gout[None], gain_share, mine.reshape(checkpoints.shape)


def solution(mesh):
    in_specs = (
        P("section", None, None, "dp"),
        P("section", None),
        P("section", None, "dp"),
        P("section", "dp", None),
        P(None, None, "dp"),
    )
    out_specs = (
        P("section", None, "dp"),
        P("section", "dp", None),
        P("section", "dp"),
        P("section", None, None, "dp"),
    )
    return jax.shard_map(shards, mesh=mesh, in_specs=in_specs, out_specs=out_specs, check_vma=False)
```

```python
import functools

import jax
import jax.numpy as jnp
from jax import lax
from jax.experimental import pallas as pl
from jax.experimental.pallas import tpu as pltpu
from jax.sharding import PartitionSpec as P

MESH = pl.DeviceIdType.MESH
F32 = jnp.float32
BF16 = jnp.bfloat16
K0 = 0.7978845608028654
K1 = 0.044715
SUB = 4
P1, P2, P3 = 0, 3, 8
A, B1, B2, E = (5, 3), (7, 6), (10, 7), (12, 9)
LAG = 0
ORDER = ('B2', 'A', 'B1', 'G', 'P3', 'P2', 'E', 'P1')
FAR_FIRST = (8, 7, 9, 6, 10, 5, 11, 4, 12, 3, 13, 2, 14, 1, 15)


def dot_nn(a, b):
    return lax.dot_general(a, b, (((1,), (0,)), ((), ())), preferred_element_type=F32)


def dot_tn(a, b):
    return lax.dot_general(a, b, (((0,), (0,)), ((), ())), preferred_element_type=F32)


def chain(
    sizes,
    x_in, cot_ref, gain_ref, win_hbm, wout_hbm,
    hid, dact, ub, dy, gg_ref, dxo_ref,
    win_ref, wout_ref, win_t, wout_t, x_ref,
    xsib, xs, xg, shin, rs, qs, dxs, dxsib,
    a1s, a1r, a2s, a2r, apart, sqs, act, slope, rb,
    d1s, d1r, d2s, d2r, dpart, ggacc, ggr, zr,
    sem1, semw,
):
    waves, rows, width, quarter, hidden, sections, peers = sizes
    half = rows // 2
    s = lax.axis_index("section")
    d = lax.axis_index("dp")
    layer, j = s // 4, s % 4
    top = sections // 4 - 1
    is_top = layer == top
    g, c = d // 2, d % 2
    sib = d + 1 - 2 * c
    near = s + 1 - 2 * (s % 2)
    far = s + 2 - 4 * ((s // 2) % 2)
    below = (s + sections - 4) % sections
    above = (s + 4) % sections

    SX, RX, SC, SG, RG, LI, LO = range(7)
    (S_XG, R_XG, S_A1, R_A1, S_A2, R_A2, S_SH, R_SH, S_DY, R_DY,
     S_D1, R_D1, S_D2, R_D2, S_RS, R_RS, S_SP, R_SP, S_Z, R_Z) = range(20)

    def at(section, dp):
        return {"section": section, "dp": dp}

    def remote(src, dst, send, recv, section, dp):
        return pltpu.make_async_remote_copy(
            src_ref=src, dst_ref=dst, send_sem=send, recv_sem=recv,
            device_id=at(section, dp), device_id_type=MESH,
        )

    def take(ref, sem):
        pltpu.make_async_copy(ref, ref, sem).wait()

    load_in = pltpu.make_async_copy(win_hbm, win_ref, sem1.at[LI])
    load_out = pltpu.make_async_copy(wout_hbm, wout_ref, sem1.at[LO])
    load_in.start()
    load_out.start()

    share = x_in.shape[2]
    wide = jnp.concatenate([x_in[...], x_in[...]], axis=-1)
    lane = lax.broadcasted_iota(jnp.int32, wide.shape, 2)
    x_ref[...] = jnp.where((lane >= share) == (c == 1), wide, jnp.zeros_like(wide))

    barrier = pltpu.get_barrier_semaphore()
    for k in range(1, peers):
        pl.semaphore_signal(barrier, inc=1, device_id=at(s, (d + k) % peers), device_id_type=MESH)
    for other in (near, far, s - j + 3 - j, below, above):
        pl.semaphore_signal(barrier, inc=1, device_id=at(other, d), device_id_type=MESH)
    pl.semaphore_wait(barrier, peers + 4)

    own_rows = pl.ds(pl.multiple_of(c * half, half), half)
    other_rows = pl.ds(pl.multiple_of((1 - c) * half, half), half)
    own_cols = pl.ds(pl.multiple_of(g * 128, 128), 128)

    pair = remote(x_ref, xsib, sem1.at[SX], sem1.at[RX], s, sib)
    pair.start()

    per = width // quarter
    q = d % per
    holds_cot = (layer == top) & (d // per == j)

    def cot_copies(w, start):
        for b in range(2):
            for hf in range(2):
                owner = q * 4 + b * 2 + hf
                src = cot_ref.at[w, pl.ds(hf * half, half), pl.ds(b * 128, 128)]
                dst = shin.at[w]

                if start:
                    @pl.when(owner == d)
                    def _():
                        pltpu.make_async_copy(src, dst, semw.at[R_SH, w]).start()

                @pl.when(owner != d)
                def _():
                    copy = remote(src, dst, sem1.at[SC], semw.at[R_SH, w], s, owner)
                    if start:
                        copy.start()
                    else:
                        copy.wait_send()

    @pl.when(holds_cot)
    def _():
        @pl.loop(0, waves)
        def _(w):
            cot_copies(w, True)

    def to_everyone(src, buf, send, recv, w):
        dst = buf.at[w, own_rows, own_cols]
        for k in FAR_FIRST:
            remote(src, dst, semw.at[send, w], semw.at[recv, w], s, (d + k) % peers).start()
        pltpu.make_async_copy(src, dst, semw.at[recv, w]).start()

    pair.wait_recv()

    @pl.loop(0, waves)
    def _(w):
        xs[w] = x_ref[w] + xsib[w]
        to_everyone(xs.at[w, own_rows], xg, S_XG, R_XG, w)

    ggacc[...] = jnp.zeros_like(ggacc)
    load_in.wait()
    load_out.wait()
    win_t[...] = win_ref[...].T
    wout_t[...] = wout_ref[...].T

    def stage_p1(w):
        take(xg.at[w], semw.at[R_XG, w])
        gain = gain_ref[...]
        xf = xg[w].astype(F32)
        sq = jnp.sum(xf * xf, axis=-1, keepdims=True)
        sq = jnp.broadcast_to(sq, (rows, 128))
        part = dot_nn((xf * gain).astype(BF16), win_ref[...])
        apart[w] = part
        sqs[w] = sq
        a1s[w, :, :hidden] = part.astype(BF16)
        a1s[w, :, hidden:] = sq.astype(BF16)
        remote(a1s.at[w], a1r.at[w], semw.at[S_A1, w], semw.at[R_A1, w], near, d).start()

    def stage_p2(w):
        take(a1r.at[w], semw.at[R_A1, w])
        part = apart[w] + a1r[w, :, :hidden].astype(F32)
        sq = sqs[w] + a1r[w, :, hidden:].astype(F32)
        apart[w] = part
        sqs[w] = sq
        a2s[w, :, :hidden] = part.astype(BF16)
        a2s[w, :, hidden:] = sq.astype(BF16)
        remote(a2s.at[w], a2r.at[w], semw.at[S_A2, w], semw.at[R_A2, w], far, d).start()

    def stage_p3(w):
        take(a2r.at[w], semw.at[R_A2, w])
        gain = gain_ref[...]
        part = apart[w] + a2r[w, :, :hidden].astype(F32)
        sq = sqs[w] + a2r[w, :, hidden:].astype(F32)
        r = lax.rsqrt(sq / width + 1e-06)
        rb[w] = r
        r1 = r[:, :1]
        a = part * r1
        t = jnp.tanh(K0 * (a + K1 * a * a * a))
        act[w] = a
        hid[w] = (0.5 * a * (1.0 + t)).astype(BF16)
        slope[w] = 0.5 * (1.0 + t) + 0.5 * a * (1.0 - t * t) * (K0 * (1.0 + 3.0 * K1 * a * a))
        ub[w] = (xg[w].astype(F32) * r1 * gain).astype(BF16)

    def stage_g(w):
        take(shin.at[w], semw.at[R_SH, w])
        to_everyone(shin.at[w], dy, S_DY, R_DY, w)

    def stage_a(w):
        take(dy.at[w], semw.at[R_DY, w])
        part = dot_nn(dy[w], wout_t[...])
        dpart[w] = part
        d1s[w] = part.astype(BF16)

        @pl.when(is_top)
        def _():
            remote(d1s.at[w], d1r.at[w], semw.at[S_D1, w], semw.at[R_D1, w], near, d).start()

        @pl.when(layer != top)
        def _():
            for to in (3 - 3 * (j // 2), 2 - j // 2, j + 1 - 2 * (j % 2)):
                slot = (to - j + 3) % 4
                remote(d1s.at[w], zr.at[w, slot], semw.at[S_Z, w], semw.at[R_Z, w], s - j + to, d).start()

    def stage_b1(w):
        take(d1r.at[w], semw.at[R_D1, w])
        part = dpart[w] + d1r[w].astype(F32)
        dpart[w] = part
        d2s[w] = part.astype(BF16)
        remote(d2s.at[w], d2r.at[w], semw.at[S_D2, w], semw.at[R_D2, w], far, d).start()

    def stage_b2(w):
        @pl.when(is_top)
        def _():
            take(d2r.at[w], semw.at[R_D2, w])
            dpart[w] = dpart[w] + d2r[w].astype(F32)

        @pl.when(layer != top)
        def _():
            take(zr.at[w], semw.at[R_Z, w])
            dpart[w] = dpart[w] + zr[w, 0].astype(F32) + zr[w, 1].astype(F32) + zr[w, 2].astype(F32)

        gain = gain_ref[...]
        dh = dpart[w]
        da = (slope[w] * dh).astype(BF16)
        dact[w] = da
        r1 = rb[w, :, :1]
        mean = jnp.sum(da.astype(F32) * act[w], axis=-1, keepdims=True) / width
        p = dot_nn(da, win_t[...])
        n = xg[w].astype(F32) * r1
        qs[w] = ((p * gain - n * mean) * r1).astype(BF16)
        for k in FAR_FIRST:
            e = (d + k) % peers
            src = qs.at[w, pl.ds(pl.multiple_of(e % 2 * half, half), half),
                        pl.ds(pl.multiple_of(e // 2 * 128, 128), 128)]
            remote(src, rs.at[w, k], semw.at[S_RS, w], semw.at[R_RS, w], s, e).start()
        pltpu.make_async_copy(qs.at[w, own_rows, own_cols], rs.at[w, 0], semw.at[R_RS, w]).start()
        ggacc[...] += jnp.sum((p * n).reshape(rows // 8, 8, quarter), axis=0)

        @pl.when(w == waves - 1)
        def _():
            for k in range(1, peers):
                e = (d + k) % peers
                src = ggacc.at[:, pl.ds(pl.multiple_of(e // 2 * 128, 128), 128)]
                remote(src, ggr.at[k], sem1.at[SG], sem1.at[RG], s, e).start()
            pltpu.make_async_copy(ggacc.at[:, own_cols], ggr.at[0], sem1.at[RG]).start()

    def stage_e(w):
        take(rs.at[w], semw.at[R_RS, w])
        total = dy[w, own_rows, own_cols].astype(F32)
        for k in range(peers):
            total = total + rs[w, k].astype(F32)
        total = total.astype(BF16)
        dxs[w] = total

        @pl.when(layer > 0)
        def _():
            remote(dxs.at[w], shin.at[w], semw.at[S_SH, w], semw.at[R_SH, w], below, d).start()

        remote(dxs.at[w], dxsib.at[w], semw.at[S_SP, w], semw.at[R_SP, w], s, sib).start()
        dxo_ref[w, own_rows, :] = total

    base = jnp.where(is_top, LAG, waves + P3 + 1)
    steps = waves + max(LAG + E[0], waves + P3 + 1 + E[1])

    def chain_at(pair):
        return base + jnp.where(is_top, pair[0], pair[1])

    stages = dict(
        G=(base, stage_g), A=(chain_at(A), stage_a), B1=(chain_at(B1), stage_b1),
        B2=(chain_at(B2), stage_b2), E=(chain_at(E), stage_e),
        P1=(P1, stage_p1), P2=(P2, stage_p2), P3=(P3, stage_p3),
    )

    @pl.loop(0, steps)
    def _(t):
        for start, stage in [stages[name] for name in ORDER]:
            w = t - start
            live = (w >= 0) & (w < waves)
            if stage is stage_b1:
                live = live & is_top
            pl.when(live)(functools.partial(stage, w))

    take(ggr, sem1.at[RG])
    gg = ggr[0]
    for k in range(1, peers):
        gg = gg + ggr[k]
    gg_ref[...] = gg

    pair.wait_send()
    take(ggr.at[pl.ds(1, peers - 1)], sem1.at[SG])

    @pl.when(holds_cot)
    def _():
        @pl.loop(0, waves)
        def _(w):
            cot_copies(w, False)

    @pl.loop(0, waves)
    def _(w):
        take(dxsib.at[w], semw.at[R_SP, w])
        dxo_ref[w, other_rows, :] = dxsib[w]
        for send in (S_XG, S_DY, S_RS):
            take(rs.at[w, pl.ds(1, peers - 1)], semw.at[send, w])
        take(a1s.at[w], semw.at[S_A1, w])
        take(a2s.at[w], semw.at[S_A2, w])

        @pl.when(is_top)
        def _():
            take(d1s.at[w], semw.at[S_D1, w])
            take(d2s.at[w], semw.at[S_D2, w])

        @pl.when(layer != top)
        def _():
            take(zr.at[w], semw.at[S_Z, w])

        take(dxs.at[w], semw.at[S_SP, w])

        @pl.when(layer > 0)
        def _():
            take(dxs.at[w], semw.at[S_SH, w])


def weight_grads(
    share, hid, dact, ub, dy, gg_ref, dxo_ref,
    gin_out, gout_out, gain_ref, mine_ref,
    gin, gout, sem,
):
    tokens = dxo_ref.shape[0] * dxo_ref.shape[1]
    odd = lax.axis_index("dp") % 2

    @pl.when(odd == 0)
    def _():
        gain_ref[...] = jnp.sum(gg_ref[:, :share], axis=0, keepdims=True)
        mine_ref[...] = dxo_ref[:, :, :share].reshape(tokens, share)

    @pl.when(odd == 1)
    def _():
        gain_ref[...] = jnp.sum(gg_ref[:, share:], axis=0, keepdims=True)
        mine_ref[...] = dxo_ref[:, :, share:].reshape(tokens, share)

    stores = []

    def product(left, right, result, out, first):
        part = result.shape[0] // 2
        for n in range(2):
            here = pl.ds(n * part, part)
            lhs = left[:, :, n * part:(n + 1) * part].reshape(tokens, part)
            rhs = right[...].reshape(tokens, right.shape[2])
            result[here, :] = dot_tn(lhs, rhs).astype(BF16)
            stores.append(pltpu.make_async_copy(result.at[here], out.at[here], sem.at[first + n]))
            stores[-1].start()

    product(hid, dy, gout, gout_out, 0)
    product(ub, dact, gin, gin_out, 2)
    for store in stores:
        store.wait()


def shards(checkpoints, gain, w_in, w_out, cotangent):
    sections, peers = lax.axis_size("section"), lax.axis_size("dp")
    waves, rows, share = checkpoints.shape[1:]
    tokens = waves * rows
    waves, rows = waves * SUB, rows // SUB
    quarter = share * peers
    width = 4 * quarter
    hidden = w_in.shape[2]
    half = rows // 2
    x = checkpoints[0].reshape(waves, rows, share)
    vmem = pl.BlockSpec(memory_space=pltpu.VMEM)
    anywhere = pl.BlockSpec(memory_space=pl.ANY)
    sizes = (waves, rows, width, quarter, hidden, sections, peers)

    def v(shape, kind=BF16):
        return pltpu.VMEM(shape, kind)

    def o(shape, kind=BF16):
        return jax.ShapeDtypeStruct(shape, kind)

    hid, dact, ub, dy, gg, dxo = pl.pallas_call(
        functools.partial(chain, sizes),
        out_shape=(
            pltpu.VMEM((waves, rows, hidden), BF16), pltpu.VMEM((waves, rows, hidden), BF16),
            pltpu.VMEM((waves, rows, quarter), BF16), pltpu.VMEM((waves, rows, quarter), BF16),
            pltpu.VMEM((8, 128), F32), pltpu.VMEM((waves, rows, 128), BF16),
        ),
        in_specs=[vmem] * 3 + [anywhere] * 2,
        out_specs=(vmem,) * 6,
        scratch_shapes=[
            v((quarter, hidden)), v((hidden, quarter)), v((hidden, quarter)), v((quarter, hidden)),
            v((waves, rows, 128)),
            v((waves, rows, 128)), v((waves, rows, 128)), v((waves, rows, quarter)),
            v((waves, half, 128)), v((waves, peers, half, 128)),
            v((waves, rows, quarter)), v((waves, half, 128)), v((waves, half, 128)),
            v((waves, rows, hidden + 128)), v((waves, rows, hidden + 128)),
            v((waves, rows, hidden + 128)), v((waves, rows, hidden + 128)),
            v((waves, rows, hidden), F32), v((waves, rows, 128), F32),
            v((waves, rows, hidden), F32), v((waves, rows, hidden), F32),
            v((waves, rows, 128), F32),
            v((waves, rows, hidden)), v((waves, rows, hidden)),
            v((waves, rows, hidden)), v((waves, rows, hidden)),
            v((waves, rows, hidden), F32), v((8, quarter), F32), v((peers, 8, 128), F32),
            v((waves, 3, rows, hidden)),
            pltpu.SemaphoreType.DMA((7,)), pltpu.SemaphoreType.DMA((20, waves)),
        ],
        compiler_params=pltpu.CompilerParams(collective_id=0, has_side_effects=True),
        name="chain",
    )(x, cotangent.reshape(waves, rows, -1), gain, w_in[0], w_out[0])
    gin, gout, gain_share, mine = pl.pallas_call(
        functools.partial(weight_grads, share),
        out_shape=(o((quarter, hidden)), o((hidden, quarter)), o((1, share), F32), o((tokens, share))),
        in_specs=[vmem] * 6,
        out_specs=(anywhere, anywhere, vmem, vmem),
        scratch_shapes=[
            v((quarter, hidden)), v((hidden, quarter)), pltpu.SemaphoreType.DMA((4,)),
        ],
        name="weight_grads",
    )(
        *[pltpu.with_memory_space_constraint(a, pltpu.MemorySpace.VMEM) for a in (hid, dact, ub, dy, gg, dxo)],
    )
    return gin[None], gout[None], gain_share, mine.reshape(checkpoints.shape)


def solution(mesh):
    in_specs = (
        P("section", None, None, "dp"),
        P("section", None),
        P("section", None, "dp"),
        P("section", "dp", None),
        P(None, None, "dp"),
    )
    out_specs = (
        P("section", None, "dp"),
        P("section", "dp", None),
        P("section", "dp"),
        P("section", None, None, "dp"),
    )
    return jax.shard_map(shards, mesh=mesh, in_specs=in_specs, out_specs=out_specs, check_vma=False)
```
